256 devices in a mesh: rows: 128 (over z, x, y_lo, core), grp: 2 (over y_hi).
Axes of the slice: x: 4, y: 4 (y_hi: 2, y_lo: 2; y = y_hi * 2 + y_lo), z: 8, core: 2. Of those that a mesh axis runs over, the one named last changes fastest.
Arguments:
- embeddings: bfloat16 [393216, 1024], P(('rows', 'grp')), may hold values from -6 to 6
- centroids: float32 [16384, 1024], P('rows', 'grp'), may hold values from -6 to 6
- block_lists: int32 [3072, 7], P(('rows', 'grp')), may hold values from -1 to 127, as said below
- block_counts: int32 [3072], P(('rows', 'grp')), may hold values from 1 to 7, as said below
Outputs:
- new_centroids: float32 [16384, 1024], P('rows', 'grp')
- evidence: float32 [393216], P(('rows', 'grp'))
The draws below stay inside these ranges and needn't reach their ends.
Inputs may be any that keep to these rules, and one draw needn't show every extreme that they name: `block_lists`: row block b is held by rows index r = b // 24. The first entry of its list is r; the entries j < block_counts[b] are distinct centroid block ids within cyclic distance 3 of r (modulo 128); entries from block_counts[b] on are -1. `block_counts`: all row blocks of one rows index have counts within one of each other; in every draw some rows index has all its counts equal to 7.
All inputs are finite; a program needn't handle non-finite values.
Results may differ from the reference program's by a relative error of at most 0.012.
The reference program's roundings to bfloat16 on the way (of `unit_rows`, `low_copy` and `shares`) count: a program that leaves them out, or rounds other values in their place, can miss the bound.
Values may be sent and summed in bfloat16 or wider, within the bound.
A program may use at most 128 MiB of HBM per device.

```python
import jax
import jax.numpy as jnp
from jax import lax

D = 1024
CB = 128
RB = 128
W = 3
ITERS = 2
L = 7
NCB = 128
K = 16384
ROWS = 393216
BPR = 24
NBLK = 3072


def list_draw(key):
    base_key = jax.random.fold_in(key, 11)
    key_level, key_heavy, key_extra, key_order = jax.random.split(base_key, 4)
    owner_of = jnp.arange(NBLK, dtype=jnp.int32) // BPR
    levels = jax.random.randint(key_level, (NCB,), 0, 8)
    base_load = jnp.where(levels == 0, L, jnp.where(levels < 3, 2, 1))
    heaviest = jax.random.randint(key_heavy, (), 0, NCB)
    base_load = jnp.where(jnp.arange(NCB) == heaviest, L, base_load)
    counts = jnp.minimum(base_load[owner_of] + jax.random.randint(key_extra, (NBLK,), 0, 2), L)
    others = jnp.concatenate([jnp.arange(1, W + 1), -jnp.arange(1, W + 1)]).astype(jnp.int32)
    orders = jax.vmap(lambda k: jax.random.permutation(k, 2 * W))(jax.random.split(key_order, NBLK))
    offsets = jnp.concatenate([jnp.zeros((NBLK, 1), jnp.int32), others[orders].astype(jnp.int32)], axis=1)
    block_ids = jnp.mod(owner_of[:, None] + offsets, NCB)
    slot_index = jnp.arange(L)
    id_lists = jnp.where(slot_index[None, :] < counts[:, None], block_ids, -1)
    return (id_lists.astype(jnp.int32), counts.astype(jnp.int32))


def draw_block_lists(key, part):
    return list_draw(key)[0]


def draw_block_counts(key, part):
    return list_draw(key)[1]


def shard_levels(own_key, dims, pieces, least, high):
    loudness = 1.0
    for position, parts in pieces:
        heights = jax.random.uniform(jax.random.fold_in(jax.random.fold_in(own_key, 6), position), (parts,), jnp.float32, least / len(pieces), high / len(pieces))
        loudness = loudness * jnp.repeat(jnp.exp(heights), dims[position] // parts).reshape((-1,) + (1,) * (len(dims) - 1 - position))
    return loudness


def normal_values(stream_key, dims, spread, bound, shards=(), kind=jnp.bfloat16):
    result = spread * jax.random.normal(stream_key, dims, jnp.float32)
    if shards:
        result = result * shard_levels(stream_key, dims, shards, -0.22, 0.18)
    return jnp.clip(result, -bound, bound).astype(kind)


def setup_inputs(seed: int = 0) -> dict:
    streams_of = jax.random.split(jax.random.key(seed), 5)
    return {
        "embeddings": normal_values(streams_of[0], (ROWS, D), 1.0, 6.0, ((0, 256),)),
        "centroids": normal_values(streams_of[1], (K, D), 1.0, 6.0, ((0, 128), (1, 2)), jnp.float32),
        "block_lists": draw_block_lists(jax.random.fold_in(streams_of[4], 71), 0),
        "block_counts": draw_block_counts(jax.random.fold_in(streams_of[4], 71), 0),
    }


EPS = 1e-06
TAU = 20.0

def normalize_rows(values):
    return values * lax.rsqrt(lax.optimization_barrier(jnp.mean(values * values, axis=-1, keepdims=True)) + EPS)

def reference(embeddings, centroids, block_lists, block_counts):
    unit_rows = normalize_rows(embeddings.astype(jnp.float32)).astype(jnp.bfloat16)
    current = normalize_rows(centroids)
    span = 2 * W + 1
    owner_rows = BPR * RB
    owner_of = jnp.arange(NBLK, dtype=jnp.int32) // BPR
    places = jnp.mod(block_lists - owner_of[:, None] + W, NCB)
    slot_index = jnp.arange(span, dtype=jnp.int32)
    in_count = slot_index[None, :] < block_counts[:, None]
    listed = jnp.any((places[:, :, None] == slot_index[None, None, :]) & in_count[:, :, None], axis=1)
    evidence = jnp.zeros((ROWS,), jnp.float32)
    for rounds in range(ITERS):
        low_copy = current.astype(jnp.bfloat16).reshape(NCB, CB, D)

        def owner_step(weighted, owner):
            members = lax.dynamic_slice_in_dim(unit_rows, owner * owner_rows, owner_rows)
            block_ids = jnp.mod(owner + slot_index - W, NCB).astype(jnp.int32)
            window = jnp.take(low_copy, block_ids, axis=0).reshape(span * CB, D)
            chosen = lax.dynamic_slice_in_dim(listed, owner * BPR, BPR)
            scores = jnp.dot(members, window.T, preferred_element_type=jnp.float32) * (TAU / D)
            grid = scores.reshape(BPR, RB, span, CB)
            weights = jnp.where(chosen[:, None, :, None], jnp.exp(grid), 0.0)
            totals = lax.optimization_barrier(jnp.sum(weights, axis=(2, 3)))
            shares = (weights / totals[:, :, None, None]).astype(jnp.bfloat16).reshape(owner_rows, span * CB)
            contribution = jnp.dot(shares.T, members, preferred_element_type=jnp.float32).reshape(span, CB, D)
            weighted = weighted.at[block_ids].add(contribution)
            return (weighted, jnp.log(totals).reshape(owner_rows))
        weighted, logs = lax.scan(owner_step, jnp.zeros((NCB, CB, D), jnp.float32), jnp.arange(NCB, dtype=jnp.int32))
        current = normalize_rows(weighted.reshape(K, D))
        evidence = logs.reshape(ROWS)
    return (current, evidence)
```

```python
import jax
import jax.numpy as jnp
from jax import lax
from jax.experimental import pallas as pl
from jax.experimental.pallas import tpu as pltpu
from jax.sharding import PartitionSpec as P

D = 1024
HALF = 512
CB = 128
RB = 128
W = 3
ITERS = 2
L = 7
ROWS_LOCAL = 1536
BLOCKS = ROWS_LOCAL // RB
TILE = 256
TILES = ROWS_LOCAL // TILE
CHUNK = 256
CHUNKS = ROWS_LOCAL // CHUNK

EPS = 1e-06
TAU = 20.0
MESH = pl.DeviceIdType.MESH

OWN, PAIR, BACK, AHEAD, FAR, PASS_BACK, PASS_AHEAD = range(7)
COPIES = 13
SCORE_GROUPS = ((OWN, 2), (BACK, 2), (FAR, 1), (PASS_BACK, 2))
SUM_GROUPS = ((PASS_BACK, 2), (BACK, 2), (FAR, 1), (OWN, 2))


def kernel(
    emb,
    cent,
    lists,
    counts,
    out,
    evidence,
    x,
    other_half,
    win,
    weights,
    shares,
    mask,
    total,
    parts,
    arrived,
    pair_sum,
    pair_other,
    full,
    load_sem,
    send_sem,
    recv_sem,
):
    r = lax.axis_index("rows")
    g = lax.axis_index("grp")
    core = r % 2
    pair = r + 1 - 2 * core
    back = (r + 126) % 128
    ahead = (r + 2) % 128
    far = (r + 125 + 6 * core) % 128
    mate = (r, 1 - g)

    def load(i):
        rows = pl.ds(i * CHUNK, CHUNK)
        return pltpu.make_async_copy(emb.at[rows], x.at[rows], load_sem.at[i])

    for i in range(CHUNKS):
        load(i).start()

    barrier = pltpu.get_barrier_semaphore()
    for device in ((pair, g), (back, g), (ahead, g), (far, g), mate):
        pl.semaphore_signal(barrier, inc=1, device_id=device, device_id_type=MESH)
    pl.semaphore_wait(barrier, 5)

    def remote(src, dst, number, device):
        return pltpu.make_async_remote_copy(
            src_ref=src,
            dst_ref=dst,
            send_sem=send_sem.at[number],
            recv_sem=recv_sem.at[number],
            device_id=device,
            device_id_type=MESH,
        )

    first = remote(cent, other_half, ITERS * COPIES, mate)
    first.start()

    slot_places = (
        W,
        W + 1 - 2 * core,
        W - 2,
        W + 2,
        6 * core,
        W - 1 - 2 * core,
        W + 3 - 2 * core,
    )
    ids = lists[...]
    which = lax.broadcasted_iota(jnp.int32, ids.shape, 0)
    nth = lax.broadcasted_iota(jnp.int32, ids.shape, 1)
    lengths = jnp.zeros(ids.shape, jnp.int32)
    for b in range(BLOCKS):
        lengths = jnp.where(which == b, counts[b], lengths)
    places = jnp.where(nth < lengths, (ids + (128 + W) - r) & 127, -1)
    for slot in range(L):
        hit = jnp.max(
            jnp.where(places == slot_places[slot], 1.0, 0.0), axis=1, keepdims=True
        )
        for b in range(BLOCKS):
            mask[slot, :, b * RB : (b + 1) * RB] = jnp.broadcast_to(
                hit[b : b + 1, :], (1, RB)
            )

    for i in range(CHUNKS):
        load(i).wait()

        def normalize(j, carry, i=i):
            rows = pl.ds(pl.multiple_of(i * CHUNK + j * 64, 64), 64)
            v = x[rows, :].astype(jnp.float32)
            m = jnp.mean(v * v, axis=1, keepdims=True)
            x[rows, :] = (v * lax.rsqrt(m + EPS)).astype(jnp.bfloat16)
            return carry

        lax.fori_loop(0, CHUNK // 64, normalize, 0)

    mine = pl.ds(pl.multiple_of(g * HALF, HALF), HALF)
    theirs = pl.ds(pl.multiple_of((1 - g) * HALF, HALF), HALF)
    first.wait()
    a = cent[...]
    b = other_half[...]
    m = (jnp.sum(a * a, axis=1, keepdims=True) + jnp.sum(b * b, axis=1, keepdims=True)) / D
    scale = lax.rsqrt(m + EPS)
    win[0, OWN, :, mine] = (a * scale).astype(jnp.bfloat16)
    win[0, OWN, :, theirs] = (b * scale).astype(jnp.bfloat16)

    for step in range(ITERS):
        base = step * COPIES
        own = win.at[step, OWN]

        fetch = {
            PAIR: remote(own, win.at[step, PAIR], base + 0, (pair, g)),
            AHEAD: remote(own, win.at[step, AHEAD], base + 1, (back, g)),
            BACK: remote(own, win.at[step, BACK], base + 2, (ahead, g)),
            FAR: remote(own, win.at[step, FAR], base + 3, (far, g)),
            PASS_BACK: remote(
                win.at[step, BACK], win.at[step, PASS_BACK], base + 4, (pair, g)
            ),
            PASS_AHEAD: remote(
                win.at[step, AHEAD], win.at[step, PASS_AHEAD], base + 5, (pair, g)
            ),
        }
        for slot in (AHEAD, BACK, FAR, PAIR):
            fetch[slot].start()

        total[...] = jnp.zeros_like(total)
        for start, size in SCORE_GROUPS:
            for slot in range(start, start + size):
                if slot != OWN:
                    fetch[slot].wait_recv()
                if slot == BACK:
                    fetch[PASS_BACK].start()
                if slot == AHEAD:
                    fetch[PASS_AHEAD].start()

            def score(t, carry, start=start, size=size):
                rows = pl.ds(pl.multiple_of(t * TILE, TILE), TILE)
                block = win[step, start : start + size].reshape(size * CB, D)
                s = lax.dot_general(
                    block,
                    x[rows, :],
                    (((1,), (1,)), ((), ())),
                    preferred_element_type=jnp.float32,
                )
                e = jnp.exp(s * (TAU / D))
                added = total[:, rows]
                for k in range(size):
                    w = e[k * CB : (k + 1) * CB, :] * mask[start + k, :, rows]
                    weights[start + k, :, rows] = w
                    added = added + jnp.sum(w, axis=0, keepdims=True)
                total[:, rows] = added
                return carry

            lax.fori_loop(0, TILES, score, 0)

        if step == ITERS - 1:
            evidence[...] = jnp.log(total[...])
        total[...] = 1.0 / total[...]

        returned = {
            PAIR: remote(parts.at[step, PAIR], arrived.at[step, PAIR], base + 6, (pair, g)),
            PASS_BACK: remote(
                parts.at[step, PASS_BACK], arrived.at[step, PASS_BACK], base + 7, (pair, g)
            ),
            PASS_AHEAD: remote(
                parts.at[step, PASS_AHEAD], arrived.at[step, PASS_AHEAD], base + 8, (pair, g)
            ),
            FAR: remote(parts.at[step, FAR], arrived.at[step, FAR], base + 9, (far, g)),
            BACK: remote(parts.at[step, BACK], arrived.at[step, AHEAD], base + 10, (back, g)),
            AHEAD: remote(parts.at[step, AHEAD], arrived.at[step, BACK], base + 11, (ahead, g)),
        }

        for start, size in SUM_GROUPS:

            def share(t, carry, start=start, size=size):
                rows = pl.ds(pl.multiple_of(t * TILE, TILE), TILE)
                inverse = total[:, rows]
                for k in range(size):
                    shares[start * CB + k * CB : start * CB + (k + 1) * CB, rows] = (
                        weights[start + k, :, rows] * inverse
                    ).astype(jnp.bfloat16)
                return carry

            lax.fori_loop(0, TILES, share, 0)
            if start == BACK:
                returned[PASS_BACK].wait_recv()
                returned[PASS_AHEAD].wait_recv()

            def add(t, carry, start=start, size=size):
                columns = pl.ds(pl.multiple_of(t * TILE, TILE), TILE)
                c = jnp.dot(
                    shares[start * CB : (start + size) * CB, :],
                    x[:, columns],
                    preferred_element_type=jnp.float32,
                )
                for k in range(size):
                    slot = start + k
                    piece = c[k * CB : (k + 1) * CB, :]
                    if slot == OWN:
                        full[:, columns] = piece
                        continue
                    if slot in (BACK, AHEAD):
                        passed = PASS_BACK if slot == BACK else PASS_AHEAD
                        piece = piece + arrived[step, passed, :, columns].astype(
                            jnp.float32
                        )
                    parts[step, slot, :, columns] = piece.astype(jnp.bfloat16)
                return carry

            lax.fori_loop(0, D // TILE, add, 0)
            for slot in range(start, start + size):
                if slot != OWN:
                    returned[slot].start()

        for slot in (PAIR, FAR):
            returned[slot].wait_recv()
        returned[BACK].wait_recv()
        returned[AHEAD].wait_recv()

        for j in range(CB // 32):
            rows = slice(j * 32, (j + 1) * 32)
            v = full[rows, :]
            for slot in (PAIR, FAR, BACK, AHEAD):
                v = v + arrived[step, slot, rows, :].astype(jnp.float32)
            pair_sum[step, rows, :] = v.astype(jnp.bfloat16)
        swap = remote(pair_sum.at[step], pair_other.at[step], base + 12, mate)
        swap.start()
        swap.wait_recv()
        for j in range(CB // 32):
            rows = slice(j * 32, (j + 1) * 32)
            v = pair_sum[step, rows, :].astype(jnp.float32) + pair_other[
                step, rows, :
            ].astype(jnp.float32)
            m = jnp.mean(v * v, axis=1, keepdims=True)
            v = v * lax.rsqrt(m + EPS)
            if step < ITERS - 1:
                win[step + 1, OWN, rows, :] = v.astype(jnp.bfloat16)
            else:
                full[rows, :] = v
        if step == ITERS - 1:
            out[...] = full[:, mine]

        for copy in list(fetch.values()) + list(returned.values()) + [swap]:
            copy.wait_send()


def local(embeddings, centroids, block_lists, block_counts):
    vmem = pl.BlockSpec(memory_space=pltpu.VMEM)
    copies = ITERS * COPIES + 1
    current, evidence = pl.pallas_call(
        kernel,
        out_shape=(
            jax.ShapeDtypeStruct((CB, HALF), jnp.float32),
            jax.ShapeDtypeStruct((1, ROWS_LOCAL), jnp.float32),
        ),
        in_specs=[
            pl.BlockSpec(memory_space=pl.ANY),
            vmem,
            vmem,
            pl.BlockSpec(memory_space=pltpu.SMEM),
        ],
        out_specs=(vmem, vmem),
        scratch_shapes=[
            pltpu.VMEM((ROWS_LOCAL, D), jnp.bfloat16),
            pltpu.VMEM((CB, HALF), jnp.float32),
            pltpu.VMEM((ITERS, L, CB, D), jnp.bfloat16),
            pltpu.VMEM((L, CB, ROWS_LOCAL), jnp.float32),
            pltpu.VMEM((L * CB, ROWS_LOCAL), jnp.bfloat16),
            pltpu.VMEM((L, 1, ROWS_LOCAL), jnp.float32),
            pltpu.VMEM((1, ROWS_LOCAL), jnp.float32),
            pltpu.VMEM((ITERS, L, CB, D), jnp.bfloat16),
            pltpu.VMEM((ITERS, L, CB, D), jnp.bfloat16),
            pltpu.VMEM((ITERS, CB, D), jnp.bfloat16),
            pltpu.VMEM((ITERS, CB, D), jnp.bfloat16),
            pltpu.VMEM((CB, D), jnp.float32),
            pltpu.SemaphoreType.DMA((CHUNKS,)),
            pltpu.SemaphoreType.DMA((copies,)),
            pltpu.SemaphoreType.DMA((copies,)),
        ],
        compiler_params=pltpu.CompilerParams(
            collective_id=0, has_side_effects=True, vmem_limit_bytes=60 * 1024 * 1024
        ),
        name="kmeans",
    )(embeddings, centroids, block_lists, block_counts)
    return (current, evidence.reshape(ROWS_LOCAL))


def solution(mesh):
    return jax.shard_map(
        local,
        mesh=mesh,
        in_specs=(
            P(("rows", "grp"), None),
            P("rows", "grp"),
            P(("rows", "grp"), None),
            P(("rows", "grp")),
        ),
        out_specs=(P("rows", "grp"), P(("rows", "grp"))),
        check_vma=False,
    )
```

```python
import jax
import jax.numpy as jnp
from jax import lax
from jax.experimental import pallas as pl
from jax.experimental.pallas import tpu as pltpu
from jax.sharding import PartitionSpec as P

D = 1024
HALF = 512
CB = 128
RB = 128
W = 3
ITERS = 2
L = 7
ROWS_LOCAL = 1536
BLOCKS = ROWS_LOCAL // RB
TILE = 512
TILES = ROWS_LOCAL // TILE
PIECES = 4
PIECE = CB // PIECES
CHUNK = 256
CHUNKS = ROWS_LOCAL // CHUNK

EPS = 1e-06
TAU = 20.0
MESH = pl.DeviceIdType.MESH

OWN, PAIR, BACK, AHEAD, FAR, PASS_BACK, PASS_AHEAD = range(7)
COPIES = 12
SCORE_GROUPS = ((OWN, 2), (BACK, 2), (FAR, 1), (PASS_BACK, 2))
SUM_GROUPS = ((PASS_BACK, 2), (BACK, 2), (FAR, 1), (OWN, 2))


def kernel(
    emb,
    cent,
    lists,
    counts,
    out,
    evidence,
    x,
    xt,
    other_half,
    win,
    weights,
    shares,
    mask,
    total,
    parts,
    arrived,
    pair_sum,
    pair_other,
    full,
    hop_first,
    hop,
    load_sem,
    send_sem,
    recv_sem,
    swap_send_sem,
    swap_recv_sem,
):
    r = lax.axis_index("rows")
    g = lax.axis_index("grp")
    core = r % 2
    pair = r + 1 - 2 * core
    back = (r + 126) % 128
    ahead = (r + 2) % 128
    far = (r + 125 + 6 * core) % 128
    beside = r + 2 - 4 * (r % 4 // 2)
    same_side = (beside, g)
    other_side = (beside, 1 - g)

    def load(i):
        rows = pl.ds(i * CHUNK, CHUNK)
        return pltpu.make_async_copy(emb.at[rows], x.at[rows], load_sem.at[i])

    for i in range(CHUNKS):
        load(i).start()

    barrier = pltpu.get_barrier_semaphore()
    for device in ((pair, g), (back, g), (ahead, g), (far, g), other_side):
        pl.semaphore_signal(barrier, inc=1, device_id=device, device_id_type=MESH)
    pl.semaphore_wait(barrier, 5)

    def remote(src, dst, number, device):
        return pltpu.make_async_remote_copy(
            src_ref=src,
            dst_ref=dst,
            send_sem=send_sem.at[number],
            recv_sem=recv_sem.at[number],
            device_id=device,
            device_id_type=MESH,
        )

    def swap_copy(src, dst, number, device):
        return pltpu.make_async_remote_copy(
            src_ref=src,
            dst_ref=dst,
            send_sem=swap_send_sem.at[number],
            recv_sem=swap_recv_sem.at[number],
            device_id=device,
            device_id_type=MESH,
        )

    def swap(src, middle, dst, turn):
        out_hops, in_hops = [], []
        for j in range(PIECES):
            rows = pl.ds(j * PIECE, PIECE)
            number = (turn * PIECES + j) * 2
            ways = (same_side, other_side) if j % 2 == 0 else (other_side, same_side)
            out_hops.append(swap_copy(src.at[rows], middle.at[rows], number, ways[0]))
            in_hops.append(swap_copy(middle.at[rows], dst.at[rows], number + 1, ways[1]))
        return out_hops, in_hops

    first_out, first_in = swap(cent, hop_first, other_half, ITERS)
    for copy in first_out:
        copy.start()

    slot_places = (
        W,
        W + 1 - 2 * core,
        W - 2,
        W + 2,
        6 * core,
        W - 1 - 2 * core,
        W + 3 - 2 * core,
    )
    ids = lists[...]
    which = lax.broadcasted_iota(jnp.int32, ids.shape, 0)
    nth = lax.broadcasted_iota(jnp.int32, ids.shape, 1)
    lengths = jnp.zeros(ids.shape, jnp.int32)
    for b in range(BLOCKS):
        lengths = jnp.where(which == b, counts[b], lengths)
    places = jnp.where(nth < lengths, (ids + (128 + W) - r) & 127, -1)
    for slot in range(L):
        hit = jnp.max(
            jnp.where(places == slot_places[slot], 1.0, 0.0), axis=1, keepdims=True
        )
        for b in range(BLOCKS):
            mask[slot, :, b * RB : (b + 1) * RB] = jnp.broadcast_to(
                hit[b : b + 1, :], (1, RB)
            )

    for j in range(PIECES):
        first_out[j].wait_recv()
        first_in[j].start()

    for i in range(CHUNKS):
        load(i).wait()

        def normalize(j, carry, i=i):
            rows = pl.ds(pl.multiple_of(i * CHUNK + j * 128, 128), 128)
            v = x[rows, :].astype(jnp.float32)
            m = jnp.mean(v * v, axis=1, keepdims=True)
            y = (v * lax.rsqrt(m + EPS)).astype(jnp.bfloat16)
            x[rows, :] = y
            xt[:, rows] = y.T
            return carry

        lax.fori_loop(0, CHUNK // 128, normalize, 0)

    mine = pl.ds(pl.multiple_of(g * HALF, HALF), HALF)
    theirs = pl.ds(pl.multiple_of((1 - g) * HALF, HALF), HALF)
    for copy in first_in:
        copy.wait_recv()
    a = cent[...]
    b = other_half[...]
    m = (jnp.sum(a * a, axis=1, keepdims=True) + jnp.sum(b * b, axis=1, keepdims=True)) / D
    scale = lax.rsqrt(m + EPS)
    win[0, OWN, :, mine] = (a * scale).astype(jnp.bfloat16)
    win[0, OWN, :, theirs] = (b * scale).astype(jnp.bfloat16)

    for step in range(ITERS):
        base = step * COPIES
        own = win.at[step, OWN]

        fetch = {
            PAIR: remote(own, win.at[step, PAIR], base + 0, (pair, g)),
            AHEAD: remote(own, win.at[step, AHEAD], base + 1, (back, g)),
            BACK: remote(own, win.at[step, BACK], base + 2, (ahead, g)),
            FAR: remote(own, win.at[step, FAR], base + 3, (far, g)),
            PASS_BACK: remote(
                win.at[step, BACK], win.at[step, PASS_BACK], base + 4, (pair, g)
            ),
            PASS_AHEAD: remote(
                win.at[step, AHEAD], win.at[step, PASS_AHEAD], base + 5, (pair, g)
            ),
        }
        for slot in (AHEAD, BACK, FAR, PAIR):
            fetch[slot].start()

        total[...] = jnp.zeros_like(total)
        for start, size in SCORE_GROUPS:
            for slot in range(start, start + size):
                if slot != OWN:
                    fetch[slot].wait_recv()
                if slot == BACK:
                    fetch[PASS_BACK].start()
                if slot == AHEAD:
                    fetch[PASS_AHEAD].start()

            def score(t, carry, start=start, size=size):
                rows = pl.ds(pl.multiple_of(t * TILE, TILE), TILE)
                block = win[step, start : start + size].reshape(size * CB, D)
                s = lax.dot_general(
                    block,
                    xt[:, rows],
                    (((1,), (0,)), ((), ())),
                    preferred_element_type=jnp.float32,
                )
                e = jnp.exp(s * (TAU / D))
                added = total[:, rows]
                for k in range(size):
                    w = e[k * CB : (k + 1) * CB, :] * mask[start + k, :, rows]
                    weights[start + k, :, rows] = w
                    added = added + jnp.sum(w, axis=0, keepdims=True)
                total[:, rows] = added
                return carry

            lax.fori_loop(0, TILES, score, 0)

        if step == ITERS - 1:
            evidence[...] = jnp.log(total[...])
        total[...] = 1.0 / total[...]

        returned = {
            PAIR: remote(parts.at[step, PAIR], arrived.at[step, PAIR], base + 6, (pair, g)),
            PASS_BACK: remote(
                parts.at[step, PASS_BACK], arrived.at[step, PASS_BACK], base + 7, (pair, g)
            ),
            PASS_AHEAD: remote(
                parts.at[step, PASS_AHEAD], arrived.at[step, PASS_AHEAD], base + 8, (pair, g)
            ),
            FAR: remote(parts.at[step, FAR], arrived.at[step, FAR], base + 9, (far, g)),
            BACK: remote(parts.at[step, BACK], arrived.at[step, AHEAD], base + 10, (back, g)),
            AHEAD: remote(parts.at[step, AHEAD], arrived.at[step, BACK], base + 11, (ahead, g)),
        }

        for start, size in SUM_GROUPS:

            def share(t, carry, start=start, size=size):
                rows = pl.ds(pl.multiple_of(t * TILE, TILE), TILE)
                inverse = total[:, rows]
                for k in range(size):
                    shares[start * CB + k * CB : start * CB + (k + 1) * CB, rows] = (
                        weights[start + k, :, rows] * inverse
                    ).astype(jnp.bfloat16)
                return carry

            lax.fori_loop(0, TILES, share, 0)
            if start == BACK:
                returned[PASS_BACK].wait_recv()
                returned[PASS_AHEAD].wait_recv()

            def add(t, carry, start=start, size=size):
                columns = pl.ds(pl.multiple_of(t * TILE, TILE), TILE)
                c = jnp.dot(
                    shares[start * CB : (start + size) * CB, :],
                    x[:, columns],
                    preferred_element_type=jnp.float32,
                )
                for k in range(size):
                    slot = start + k
                    piece = c[k * CB : (k + 1) * CB, :]
                    if slot == OWN:
                        full[:, columns] = piece
                        continue
                    if slot in (BACK, AHEAD):
                        passed = PASS_BACK if slot == BACK else PASS_AHEAD
                        piece = piece + arrived[step, passed, :, columns].astype(
                            jnp.float32
                        )
                    parts[step, slot, :, columns] = piece.astype(jnp.bfloat16)
                return carry

            lax.fori_loop(0, D // TILE, add, 0)
            for slot in range(start, start + size):
                if slot != OWN:
                    returned[slot].start()

        for slot in (PAIR, FAR):
            returned[slot].wait_recv()
        returned[BACK].wait_recv()
        returned[AHEAD].wait_recv()

        swap_out, swap_in = swap(
            pair_sum.at[step], hop.at[step], pair_other.at[step], step
        )
        for j in range(PIECES):
            rows = slice(j * PIECE, (j + 1) * PIECE)
            v = full[rows, :]
            for slot in (PAIR, FAR, BACK, AHEAD):
                v = v + arrived[step, slot, rows, :].astype(jnp.float32)
            pair_sum[step, rows, :] = v.astype(jnp.bfloat16)
            swap_out[j].start()
        for j in range(PIECES):
            swap_out[j].wait_recv()
            swap_in[j].start()
        for j in range(PIECES):
            rows = slice(j * PIECE, (j + 1) * PIECE)
            swap_in[j].wait_recv()
            v = pair_sum[step, rows, :].astype(jnp.float32) + pair_other[
                step, rows, :
            ].astype(jnp.float32)
            m = jnp.mean(v * v, axis=1, keepdims=True)
            v = v * lax.rsqrt(m + EPS)
            if step < ITERS - 1:
                win[step + 1, OWN, rows, :] = v.astype(jnp.bfloat16)
            else:
                full[rows, :] = v
        if step == ITERS - 1:
            out[...] = full[:, mine]

        for copy in list(fetch.values()) + list(returned.values()) + swap_out + swap_in:
            copy.wait_send()

    for copy in first_out + first_in:
        copy.wait_send()


def local(embeddings, centroids, block_lists, block_counts):
    vmem = pl.BlockSpec(memory_space=pltpu.VMEM)
    copies = ITERS * COPIES
    swaps = (ITERS + 1) * PIECES * 2
    current, evidence = pl.pallas_call(
        kernel,
        out_shape=(
            jax.ShapeDtypeStruct((CB, HALF), jnp.float32),
            jax.ShapeDtypeStruct((1, ROWS_LOCAL), jnp.float32),
        ),
        in_specs=[
            pl.BlockSpec(memory_space=pl.ANY),
            vmem,
            vmem,
            pl.BlockSpec(memory_space=pltpu.SMEM),
        ],
        out_specs=(vmem, vmem),
        scratch_shapes=[
            pltpu.VMEM((ROWS_LOCAL, D), jnp.bfloat16),
            pltpu.VMEM((D, ROWS_LOCAL), jnp.bfloat16),
            pltpu.VMEM((CB, HALF), jnp.float32),
            pltpu.VMEM((ITERS, L, CB, D), jnp.bfloat16),
            pltpu.VMEM((L, CB, ROWS_LOCAL), jnp.float32),
            pltpu.VMEM((L * CB, ROWS_LOCAL), jnp.bfloat16),
            pltpu.VMEM((L, 1, ROWS_LOCAL), jnp.float32),
            pltpu.VMEM((1, ROWS_LOCAL), jnp.float32),
            pltpu.VMEM((ITERS, L, CB, D), jnp.bfloat16),
            pltpu.VMEM((ITERS, L, CB, D), jnp.bfloat16),
            pltpu.VMEM((ITERS, CB, D), jnp.bfloat16),
            pltpu.VMEM((ITERS, CB, D), jnp.bfloat16),
            pltpu.VMEM((CB, D), jnp.float32),
            pltpu.VMEM((CB, HALF), jnp.float32),
            pltpu.VMEM((ITERS, CB, D), jnp.bfloat16),
            pltpu.SemaphoreType.DMA((CHUNKS,)),
            pltpu.SemaphoreType.DMA((copies,)),
            pltpu.SemaphoreType.DMA((copies,)),
            pltpu.SemaphoreType.DMA((swaps,)),
            pltpu.SemaphoreType.DMA((swaps,)),
        ],
        compiler_params=pltpu.CompilerParams(
            collective_id=0, has_side_effects=True, vmem_limit_bytes=60 * 1024 * 1024
        ),
        name="kmeans",
    )(embeddings, centroids, block_lists, block_counts)
    return (current, evidence.reshape(ROWS_LOCAL))


def solution(mesh):
    return jax.shard_map(
        local,
        mesh=mesh,
        in_specs=(
            P(("rows", "grp"), None),
            P("rows", "grp"),
            P(("rows", "grp"), None),
            P(("rows", "grp")),
        ),
        out_specs=(P("rows", "grp"), P(("rows", "grp"))),
        check_vma=False,
    )
```

```python
import jax
import jax.numpy as jnp
from jax import lax
from jax.experimental import pallas as pl
from jax.experimental.pallas import tpu as pltpu
from jax.sharding import PartitionSpec as P

D = 1024
HALF = 512
CB = 128
RB = 128
W = 3
ITERS = 2
L = 7
ROWS_LOCAL = 1536
BLOCKS = ROWS_LOCAL // RB
TILE = 768
TILES = ROWS_LOCAL // TILE
COLUMNS = 1024
PIECES = 4
PIECE = CB // PIECES
CHUNK = 256
CHUNKS = ROWS_LOCAL // CHUNK

EPS = 1e-06
TAU = 20.0
MESH = pl.DeviceIdType.MESH

OWN, PAIR, BACK, AHEAD, FAR, PASS_BACK, PASS_AHEAD = range(7)
COPIES = 12
SCORE_GROUPS = ((OWN, 2), (FAR, 1), (BACK, 2), (PASS_BACK, 2))
SUM_GROUPS = ((PASS_BACK, 2), (BACK, 2), (FAR, 1), (OWN, 2))


def kernel(
    emb,
    cent,
    lists,
    counts,
    out,
    evidence,
    x,
    xt,
    other_half,
    win,
    weights,
    shares,
    mask,
    total,
    parts,
    arrived,
    pair_sum,
    pair_other,
    full,
    load_sem,
    send_sem,
    recv_sem,
    swap_send_sem,
    swap_recv_sem,
):
    r = lax.axis_index("rows")
    g = lax.axis_index("grp")
    core = r % 2
    pair = r + 1 - 2 * core
    back = (r + 126) % 128
    ahead = (r + 2) % 128
    far = (r + 125 + 6 * core) % 128
    mate = (r, 1 - g)
    low = r % 4 // 2
    back_at = (back, (g + 1 - low) % 2)
    ahead_at = (ahead, (g + low) % 2)

    def load(i):
        rows = pl.ds(i * CHUNK, CHUNK)
        return pltpu.make_async_copy(emb.at[rows], x.at[rows], load_sem.at[i])

    for i in range(CHUNKS):
        load(i).start()

    barrier = pltpu.get_barrier_semaphore()
    for device in ((pair, g), back_at, ahead_at, (far, g), mate):
        pl.semaphore_signal(barrier, inc=1, device_id=device, device_id_type=MESH)
    pl.semaphore_wait(barrier, 5)

    def remote(src, dst, number, device):
        return pltpu.make_async_remote_copy(
            src_ref=src,
            dst_ref=dst,
            send_sem=send_sem.at[number],
            recv_sem=recv_sem.at[number],
            device_id=device,
            device_id_type=MESH,
        )

    def swap_copy(src, dst, number, device):
        return pltpu.make_async_remote_copy(
            src_ref=src,
            dst_ref=dst,
            send_sem=swap_send_sem.at[number],
            recv_sem=swap_recv_sem.at[number],
            device_id=device,
            device_id_type=MESH,
        )

    def swap(src, dst, turn):
        return [
            swap_copy(
                src.at[pl.ds(j * PIECE, PIECE)],
                dst.at[pl.ds(j * PIECE, PIECE)],
                turn * PIECES + j,
                mate,
            )
            for j in range(PIECES)
        ]

    first = swap(cent, other_half, ITERS)
    for copy in first:
        copy.start()

    slot_places = (
        W,
        W + 1 - 2 * core,
        W - 2,
        W + 2,
        6 * core,
        W - 1 - 2 * core,
        W + 3 - 2 * core,
    )
    ids = lists[...]
    which = lax.broadcasted_iota(jnp.int32, ids.shape, 0)
    nth = lax.broadcasted_iota(jnp.int32, ids.shape, 1)
    lengths = jnp.zeros(ids.shape, jnp.int32)
    for b in range(BLOCKS):
        lengths = jnp.where(which == b, counts[b], lengths)
    places = jnp.where(nth < lengths, (ids + (128 + W) - r) & 127, -1)
    for slot in range(L):
        hit = jnp.max(
            jnp.where(places == slot_places[slot], 1.0, 0.0), axis=1, keepdims=True
        )
        for b in range(BLOCKS):
            mask[slot, :, b * RB : (b + 1) * RB] = jnp.broadcast_to(
                hit[b : b + 1, :], (1, RB)
            )

    for i in range(CHUNKS):
        load(i).wait()

        def normalize(j, carry, i=i):
            rows = pl.ds(pl.multiple_of(i * CHUNK + j * 128, 128), 128)
            v = x[rows, :].astype(jnp.float32)
            m = jnp.mean(v * v, axis=1, keepdims=True)
            y = (v * lax.rsqrt(m + EPS)).astype(jnp.bfloat16)
            x[rows, :] = y
            xt[:, rows] = y.T
            return carry

        lax.fori_loop(0, CHUNK // 128, normalize, 0)

    mine = pl.ds(pl.multiple_of(g * HALF, HALF), HALF)
    theirs = pl.ds(pl.multiple_of((1 - g) * HALF, HALF), HALF)
    for copy in first:
        copy.wait_recv()
    a = cent[...]
    b = other_half[...]
    m = (jnp.sum(a * a, axis=1, keepdims=True) + jnp.sum(b * b, axis=1, keepdims=True)) / D
    scale = lax.rsqrt(m + EPS)
    win[0, OWN, :, mine] = (a * scale).astype(jnp.bfloat16)
    win[0, OWN, :, theirs] = (b * scale).astype(jnp.bfloat16)

    for step in range(ITERS):
        base = step * COPIES
        own = win.at[step, OWN]

        fetch = {
            PAIR: remote(own, win.at[step, PAIR], base + 0, (pair, g)),
            AHEAD: remote(own, win.at[step, AHEAD], base + 1, back_at),
            BACK: remote(own, win.at[step, BACK], base + 2, ahead_at),
            FAR: remote(own, win.at[step, FAR], base + 3, (far, g)),
            PASS_BACK: remote(
                win.at[step, BACK], win.at[step, PASS_BACK], base + 4, (pair, g)
            ),
            PASS_AHEAD: remote(
                win.at[step, AHEAD], win.at[step, PASS_AHEAD], base + 5, (pair, g)
            ),
        }
        for slot in (AHEAD, BACK, FAR, PAIR):
            fetch[slot].start()

        total[...] = jnp.zeros_like(total)
        for start, size in SCORE_GROUPS:
            for slot in range(start, start + size):
                if slot != OWN:
                    fetch[slot].wait_recv()
                if slot == BACK:
                    fetch[PASS_BACK].start()
                if slot == AHEAD:
                    fetch[PASS_AHEAD].start()

            def score(t, carry, start=start, size=size):
                rows = pl.ds(pl.multiple_of(t * TILE, TILE), TILE)
                block = win[step, start : start + size].reshape(size * CB, D)
                s = lax.dot_general(
                    block,
                    xt[:, rows],
                    (((1,), (0,)), ((), ())),
                    preferred_element_type=jnp.float32,
                )
                e = jnp.exp(s * (TAU / D))
                added = total[:, rows]
                for k in range(size):
                    w = e[k * CB : (k + 1) * CB, :] * mask[start + k, :, rows]
                    weights[start + k, :, rows] = w
                    added = added + jnp.sum(w, axis=0, keepdims=True)
                total[:, rows] = added
                return carry

            lax.fori_loop(0, TILES, score, 0)

        if step == ITERS - 1:
            evidence[...] = jnp.log(total[...])
        total[...] = 1.0 / total[...]

        returned = {
            PAIR: remote(parts.at[step, PAIR], arrived.at[step, PAIR], base + 6, (pair, g)),
            PASS_BACK: remote(
                parts.at[step, PASS_BACK], arrived.at[step, PASS_BACK], base + 7, (pair, g)
            ),
            PASS_AHEAD: remote(
                parts.at[step, PASS_AHEAD], arrived.at[step, PASS_AHEAD], base + 8, (pair, g)
            ),
            FAR: remote(parts.at[step, FAR], arrived.at[step, FAR], base + 9, (far, g)),
            BACK: remote(parts.at[step, BACK], arrived.at[step, AHEAD], base + 10, back_at),
            AHEAD: remote(parts.at[step, AHEAD], arrived.at[step, BACK], base + 11, ahead_at),
        }

        for start, size in SUM_GROUPS:

            def share(t, carry, start=start, size=size):
                rows = pl.ds(pl.multiple_of(t * TILE, TILE), TILE)
                inverse = total[:, rows]
                for k in range(size):
                    shares[start * CB + k * CB : start * CB + (k + 1) * CB, rows] = (
                        weights[start + k, :, rows] * inverse
                    ).astype(jnp.bfloat16)
                return carry

            lax.fori_loop(0, TILES, share, 0)
            if start == BACK:
                returned[PASS_BACK].wait_recv()
                returned[PASS_AHEAD].wait_recv()

            def add(t, carry, start=start, size=size):
                columns = pl.ds(pl.multiple_of(t * COLUMNS, COLUMNS), COLUMNS)
                c = jnp.dot(
                    shares[start * CB : (start + size) * CB, :],
                    x[:, columns],
                    preferred_element_type=jnp.float32,
                )
                for k in range(size):
                    slot = start + k
                    piece = c[k * CB : (k + 1) * CB, :]
                    if slot == OWN:
                        full[:, columns] = piece
                        continue
                    if slot in (BACK, AHEAD):
                        passed = PASS_BACK if slot == BACK else PASS_AHEAD
                        piece = piece + arrived[step, passed, :, columns].astype(
                            jnp.float32
                        )
                    parts[step, slot, :, columns] = piece.astype(jnp.bfloat16)
                return carry

            lax.fori_loop(0, D // COLUMNS, add, 0)
            for slot in range(start, start + size):
                if slot != OWN:
                    returned[slot].start()

        for slot in (PAIR, FAR):
            returned[slot].wait_recv()
        returned[BACK].wait_recv()
        returned[AHEAD].wait_recv()

        swaps = swap(pair_sum.at[step], pair_other.at[step], step)
        for j in range(PIECES):
            rows = slice(j * PIECE, (j + 1) * PIECE)
            v = full[rows, :]
            for slot in (PAIR, FAR, BACK, AHEAD):
                v = v + arrived[step, slot, rows, :].astype(jnp.float32)
            pair_sum[step, rows, :] = v.astype(jnp.bfloat16)
            swaps[j].start()
        for j in range(PIECES):
            rows = slice(j * PIECE, (j + 1) * PIECE)
            swaps[j].wait_recv()
            v = pair_sum[step, rows, :].astype(jnp.float32) + pair_other[
                step, rows, :
            ].astype(jnp.float32)
            m = jnp.mean(v * v, axis=1, keepdims=True)
            v = v * lax.rsqrt(m + EPS)
            if step < ITERS - 1:
                win[step + 1, OWN, rows, :] = v.astype(jnp.bfloat16)
            else:
                full[rows, :] = v
        if step == ITERS - 1:
            out[...] = full[:, mine]

        for copy in list(fetch.values()) + list(returned.values()) + swaps:
            copy.wait_send()

    for copy in first:
        copy.wait_send()


def local(embeddings, centroids, block_lists, block_counts):
    vmem = pl.BlockSpec(memory_space=pltpu.VMEM)
    copies = ITERS * COPIES
    swaps = (ITERS + 1) * PIECES
    current, evidence = pl.pallas_call(
        kernel,
        out_shape=(
            jax.ShapeDtypeStruct((CB, HALF), jnp.float32),
            jax.ShapeDtypeStruct((1, ROWS_LOCAL), jnp.float32),
        ),
        in_specs=[
            pl.BlockSpec(memory_space=pl.ANY),
            vmem,
            vmem,
            pl.BlockSpec(memory_space=pltpu.SMEM),
        ],
        out_specs=(vmem, vmem),
        scratch_shapes=[
            pltpu.VMEM((ROWS_LOCAL, D), jnp.bfloat16),
            pltpu.VMEM((D, ROWS_LOCAL), jnp.bfloat16),
            pltpu.VMEM((CB, HALF), jnp.float32),
            pltpu.VMEM((ITERS, L, CB, D), jnp.bfloat16),
            pltpu.VMEM((L, CB, ROWS_LOCAL), jnp.float32),
            pltpu.VMEM((L * CB, ROWS_LOCAL), jnp.bfloat16),
            pltpu.VMEM((L, 1, ROWS_LOCAL), jnp.float32),
            pltpu.VMEM((1, ROWS_LOCAL), jnp.float32),
            pltpu.VMEM((ITERS, L, CB, D), jnp.bfloat16),
            pltpu.VMEM((ITERS, L, CB, D), jnp.bfloat16),
            pltpu.VMEM((ITERS, CB, D), jnp.bfloat16),
            pltpu.VMEM((ITERS, CB, D), jnp.bfloat16),
            pltpu.VMEM((CB, D), jnp.float32),
            pltpu.SemaphoreType.DMA((CHUNKS,)),
            pltpu.SemaphoreType.DMA((copies,)),
            pltpu.SemaphoreType.DMA((copies,)),
            pltpu.SemaphoreType.DMA((swaps,)),
            pltpu.SemaphoreType.DMA((swaps,)),
        ],
        compiler_params=pltpu.CompilerParams(
            collective_id=0, has_side_effects=True, vmem_limit_bytes=60 * 1024 * 1024
        ),
        name="kmeans",
    )(embeddings, centroids, block_lists, block_counts)
    return (current, evidence.reshape(ROWS_LOCAL))


def solution(mesh):
    return jax.shard_map(
        local,
        mesh=mesh,
        in_specs=(
            P(("rows", "grp"), None),
            P("rows", "grp"),
            P(("rows", "grp"), None),
            P(("rows", "grp")),
        ),
        out_specs=(P("rows", "grp"), P(("rows", "grp"))),
        check_vma=False,
    )
```

```python
import jax
import jax.numpy as jnp
from jax import lax
from jax.experimental import pallas as pl
from jax.experimental.pallas import tpu as pltpu
from jax.sharding import PartitionSpec as P

D = 1024
HALF = 512
CB = 128
RB = 128
W = 3
ITERS = 2
L = 7
ROWS_LOCAL = 1536
BLOCKS = ROWS_LOCAL // RB
TILE = 768
TILES = ROWS_LOCAL // TILE
COLUMNS = 1024
PIECES = 4
PIECE = CB // PIECES
SPAN = CB // 2
CHUNK = 256
CHUNKS = ROWS_LOCAL // CHUNK

EPS = 1e-06
TAU = 20.0
MESH = pl.DeviceIdType.MESH

OWN, PAIR, BACK, AHEAD, FAR, PASS_BACK, PASS_AHEAD = range(7)
COPIES = 12
SCORE_GROUPS = ((OWN, 2), (BACK, 2), (FAR, 1), (PASS_BACK, 2))
SUM_GROUPS = ((PASS_BACK, 2), (BACK, 2), (FAR, 1), (OWN, 2))


def kernel(
    emb,
    cent,
    lists,
    counts,
    out,
    evidence,
    x,
    xt,
    other_half,
    win,
    weights,
    shares,
    mask,
    total,
    parts,
    arrived,
    pair_sum,
    pair_other,
    full,
    load_sem,
    send_sem,
    recv_sem,
    swap_send_sem,
    swap_recv_sem,
):
    r = lax.axis_index("rows")
    g = lax.axis_index("grp")
    core = r % 2
    pair = r + 1 - 2 * core
    back = (r + 126) % 128
    ahead = (r + 2) % 128
    far = (r + 125 + 6 * core) % 128
    mate = (r, 1 - g)
    low = r % 4 // 2
    back_at = (back, (g + 1 - low) % 2)
    ahead_at = (ahead, (g + low) % 2)

    def load(i):
        rows = pl.ds(i * CHUNK, CHUNK)
        return pltpu.make_async_copy(emb.at[rows], x.at[rows], load_sem.at[i])

    for i in range(CHUNKS):
        load(i).start()

    barrier = pltpu.get_barrier_semaphore()
    for device in ((pair, g), back_at, ahead_at, (far, g), mate):
        pl.semaphore_signal(barrier, inc=1, device_id=device, device_id_type=MESH)
    pl.semaphore_wait(barrier, 5)

    def remote(src, dst, number, device):
        return pltpu.make_async_remote_copy(
            src_ref=src,
            dst_ref=dst,
            send_sem=send_sem.at[number],
            recv_sem=recv_sem.at[number],
            device_id=device,
            device_id_type=MESH,
        )

    def swap_copy(src, dst, number, device):
        return pltpu.make_async_remote_copy(
            src_ref=src,
            dst_ref=dst,
            send_sem=swap_send_sem.at[number],
            recv_sem=swap_recv_sem.at[number],
            device_id=device,
            device_id_type=MESH,
        )

    def swap(src, dst, turn):
        return [
            swap_copy(
                src.at[pl.ds(j * PIECE, PIECE)],
                dst.at[pl.ds(j * PIECE, PIECE)],
                turn * PIECES + j,
                mate,
            )
            for j in range(PIECES)
        ]

    first = swap(cent, other_half, ITERS)
    for copy in first:
        copy.start()

    slot_places = (
        W,
        W + 1 - 2 * core,
        W - 2,
        W + 2,
        6 * core,
        W - 1 - 2 * core,
        W + 3 - 2 * core,
    )
    ids = lists[...]
    which = lax.broadcasted_iota(jnp.int32, ids.shape, 0)
    nth = lax.broadcasted_iota(jnp.int32, ids.shape, 1)
    lengths = jnp.zeros(ids.shape, jnp.int32)
    for b in range(BLOCKS):
        lengths = jnp.where(which == b, counts[b], lengths)
    places = jnp.where(nth < lengths, (ids + (128 + W) - r) & 127, -1)
    for slot in range(L):
        hit = jnp.max(
            jnp.where(places == slot_places[slot], 1.0, 0.0), axis=1, keepdims=True
        )
        for b in range(BLOCKS):
            mask[slot, :, b * RB : (b + 1) * RB] = jnp.broadcast_to(
                hit[b : b + 1, :], (1, RB)
            )

    for i in range(CHUNKS):
        load(i).wait()

        def normalize(j, carry, i=i):
            rows = pl.ds(pl.multiple_of(i * CHUNK + j * 128, 128), 128)
            v = x[rows, :].astype(jnp.float32)
            m = jnp.mean(v * v, axis=1, keepdims=True)
            y = (v * lax.rsqrt(m + EPS)).astype(jnp.bfloat16)
            x[rows, :] = y
            xt[:, rows] = y.T
            return carry

        lax.fori_loop(0, CHUNK // 128, normalize, 0)

    mine = pl.ds(pl.multiple_of(g * HALF, HALF), HALF)
    theirs = pl.ds(pl.multiple_of((1 - g) * HALF, HALF), HALF)
    for copy in first:
        copy.wait_recv()
    a = cent[...]
    b = other_half[...]
    m = (jnp.sum(a * a, axis=1, keepdims=True) + jnp.sum(b * b, axis=1, keepdims=True)) / D
    scale = lax.rsqrt(m + EPS)
    win[0, OWN, :, mine] = (a * scale).astype(jnp.bfloat16)
    win[0, OWN, :, theirs] = (b * scale).astype(jnp.bfloat16)

    def halves(src, dst, number, device):
        return [
            remote(
                src.at[pl.ds(h * SPAN, SPAN)],
                dst.at[pl.ds(h * SPAN, SPAN)],
                number * 2 + h,
                device,
            )
            for h in range(2)
        ]

    fetches = []
    for step in range(ITERS):
        base = step * COPIES
        slots = [win.at[step, slot] for slot in range(L)]
        fetches.append(
            {
                PAIR: halves(slots[OWN], slots[PAIR], base + 0, (pair, g)),
                AHEAD: halves(slots[OWN], slots[AHEAD], base + 1, back_at),
                BACK: halves(slots[OWN], slots[BACK], base + 2, ahead_at),
                FAR: halves(slots[OWN], slots[FAR], base + 3, (far, g)),
                PASS_BACK: halves(slots[BACK], slots[PASS_BACK], base + 4, (pair, g)),
                PASS_AHEAD: halves(slots[AHEAD], slots[PASS_AHEAD], base + 5, (pair, g)),
            }
        )

    def start_fetch(step, h):
        for slot in (AHEAD, BACK, FAR, PAIR):
            fetches[step][slot][h].start()

    for h in range(2):
        start_fetch(0, h)

    for step in range(ITERS):
        base = step * COPIES
        fetch = fetches[step]

        total[...] = jnp.zeros_like(total)
        for start, size in SCORE_GROUPS:
            for slot in range(start, start + size):
                for h in range(2):
                    if slot != OWN:
                        fetch[slot][h].wait_recv()
                    if slot == BACK:
                        fetch[PASS_BACK][h].start()
                    if slot == AHEAD:
                        fetch[PASS_AHEAD][h].start()

            def score(t, carry, start=start, size=size):
                rows = pl.ds(pl.multiple_of(t * TILE, TILE), TILE)
                block = win[step, start : start + size].reshape(size * CB, D)
                s = lax.dot_general(
                    block,
                    xt[:, rows],
                    (((1,), (0,)), ((), ())),
                    preferred_element_type=jnp.float32,
                )
                e = jnp.exp(s * (TAU / D))
                added = total[:, rows]
                for k in range(size):
                    w = e[k * CB : (k + 1) * CB, :] * mask[start + k, :, rows]
                    weights[start + k, :, rows] = w
                    added = added + jnp.sum(w, axis=0, keepdims=True)
                total[:, rows] = added
                return carry

            lax.fori_loop(0, TILES, score, 0)

        if step == ITERS - 1:
            evidence[...] = jnp.log(total[...])
        total[...] = 1.0 / total[...]

        returned = {
            PAIR: halves(parts.at[step, PAIR], arrived.at[step, PAIR], base + 6, (pair, g)),
            PASS_BACK: halves(
                parts.at[step, PASS_BACK], arrived.at[step, PASS_BACK], base + 7, (pair, g)
            ),
            PASS_AHEAD: halves(
                parts.at[step, PASS_AHEAD], arrived.at[step, PASS_AHEAD], base + 8, (pair, g)
            ),
            FAR: halves(parts.at[step, FAR], arrived.at[step, FAR], base + 9, (far, g)),
            BACK: halves(parts.at[step, BACK], arrived.at[step, AHEAD], base + 10, back_at),
            AHEAD: halves(parts.at[step, AHEAD], arrived.at[step, BACK], base + 11, ahead_at),
        }

        for start, size in SUM_GROUPS:

            def share(t, carry, start=start, size=size):
                rows = pl.ds(pl.multiple_of(t * TILE, TILE), TILE)
                inverse = total[:, rows]
                for k in range(size):
                    shares[start * CB + k * CB : start * CB + (k + 1) * CB, rows] = (
                        weights[start + k, :, rows] * inverse
                    ).astype(jnp.bfloat16)
                return carry

            lax.fori_loop(0, TILES, share, 0)
            if start == BACK:
                for h in range(2):
                    returned[PASS_BACK][h].wait_recv()
                    returned[PASS_AHEAD][h].wait_recv()

            def add(t, carry, start=start, size=size):
                columns = pl.ds(pl.multiple_of(t * COLUMNS, COLUMNS), COLUMNS)
                c = jnp.dot(
                    shares[start * CB : (start + size) * CB, :],
                    x[:, columns],
                    preferred_element_type=jnp.float32,
                )
                for k in range(size):
                    slot = start + k
                    piece = c[k * CB : (k + 1) * CB, :]
                    if slot == OWN:
                        full[:, columns] = piece
                        continue
                    if slot in (BACK, AHEAD):
                        passed = PASS_BACK if slot == BACK else PASS_AHEAD
                        piece = piece + arrived[step, passed, :, columns].astype(
                            jnp.float32
                        )
                    parts[step, slot, :, columns] = piece.astype(jnp.bfloat16)
                return carry

            lax.fori_loop(0, D // COLUMNS, add, 0)
            for slot in range(start, start + size):
                if slot != OWN:
                    for h in range(2):
                        returned[slot][h].start()

        swaps = swap(pair_sum.at[step], pair_other.at[step], step)
        for j in range(PIECES):
            rows = slice(j * PIECE, (j + 1) * PIECE)
            if j * 2 % PIECES == 0:
                for slot in (PAIR, FAR, BACK, AHEAD):
                    returned[slot][j * 2 // PIECES].wait_recv()
            v = full[rows, :]
            for slot in (PAIR, FAR, BACK, AHEAD):
                v = v + arrived[step, slot, rows, :].astype(jnp.float32)
            pair_sum[step, rows, :] = v.astype(jnp.bfloat16)
            swaps[j].start()
        for j in range(PIECES):
            rows = slice(j * PIECE, (j + 1) * PIECE)
            swaps[j].wait_recv()
            v = pair_sum[step, rows, :].astype(jnp.float32) + pair_other[
                step, rows, :
            ].astype(jnp.float32)
            m = jnp.mean(v * v, axis=1, keepdims=True)
            v = v * lax.rsqrt(m + EPS)
            if step < ITERS - 1:
                win[step + 1, OWN, rows, :] = v.astype(jnp.bfloat16)
                if (j + 1) * 2 % PIECES == 0:
                    start_fetch(step + 1, (j + 1) * 2 // PIECES - 1)
            else:
                full[rows, :] = v
        if step == ITERS - 1:
            out[...] = full[:, mine]

        for copies in list(fetch.values()) + list(returned.values()) + [swaps]:
            for copy in copies:
                copy.wait_send()

    for copy in first:
        copy.wait_send()


def local(embeddings, centroids, block_lists, block_counts):
    vmem = pl.BlockSpec(memory_space=pltpu.VMEM)
    copies = ITERS * COPIES * 2
    swaps = (ITERS + 1) * PIECES
    current, evidence = pl.pallas_call(
        kernel,
        out_shape=(
            jax.ShapeDtypeStruct((CB, HALF), jnp.float32),
            jax.ShapeDtypeStruct((1, ROWS_LOCAL), jnp.float32),
        ),
        in_specs=[
            pl.BlockSpec(memory_space=pl.ANY),
            vmem,
            vmem,
            pl.BlockSpec(memory_space=pltpu.SMEM),
        ],
        out_specs=(vmem, vmem),
        scratch_shapes=[
            pltpu.VMEM((ROWS_LOCAL, D), jnp.bfloat16),
            pltpu.VMEM((D, ROWS_LOCAL), jnp.bfloat16),
            pltpu.VMEM((CB, HALF), jnp.float32),
            pltpu.VMEM((ITERS, L, CB, D), jnp.bfloat16),
            pltpu.VMEM((L, CB, ROWS_LOCAL), jnp.float32),
            pltpu.VMEM((L * CB, ROWS_LOCAL), jnp.bfloat16),
            pltpu.VMEM((L, 1, ROWS_LOCAL), jnp.float32),
            pltpu.VMEM((1, ROWS_LOCAL), jnp.float32),
            pltpu.VMEM((ITERS, L, CB, D), jnp.bfloat16),
            pltpu.VMEM((ITERS, L, CB, D), jnp.bfloat16),
            pltpu.VMEM((ITERS, CB, D), jnp.bfloat16),
            pltpu.VMEM((ITERS, CB, D), jnp.bfloat16),
            pltpu.VMEM((CB, D), jnp.float32),
            pltpu.SemaphoreType.DMA((CHUNKS,)),
            pltpu.SemaphoreType.DMA((copies,)),
            pltpu.SemaphoreType.DMA((copies,)),
            pltpu.SemaphoreType.DMA((swaps,)),
            pltpu.SemaphoreType.DMA((swaps,)),
        ],
        compiler_params=pltpu.CompilerParams(
            collective_id=0, has_side_effects=True, vmem_limit_bytes=60 * 1024 * 1024
        ),
        name="kmeans",
    )(embeddings, centroids, block_lists, block_counts)
    return (current, evidence.reshape(ROWS_LOCAL))


def solution(mesh):
    return jax.shard_map(
        local,
        mesh=mesh,
        in_specs=(
            P(("rows", "grp"), None),
            P("rows", "grp"),
            P(("rows", "grp"), None),
            P(("rows", "grp")),
        ),
        out_specs=(P("rows", "grp"), P(("rows", "grp"))),
        check_vma=False,
    )
```
